32 devices in a mesh: pipe: 4 (over y, x), ctx: 2 (over core), tp: 4 (over z).
Axes of the slice: x: 2, y: 2, z: 4, core: 2. Of those that a mesh axis runs over, the one named last changes fastest.
Arguments:
- fwd_acts: bfloat16 [4, 256, 16384], P('pipe', 'ctx', 'tp'), may hold values from -6 to 6
- back_grads: bfloat16 [4, 256, 16384], P('pipe', 'ctx', 'tp'), may hold values from -6 to 6
- stashed: bfloat16 [4, 3, 256, 16384], P('pipe', None, 'ctx', 'tp'), may hold values from -6 to 6
- layer_weights: bfloat16 [2, 4, 16384, 2304], P(None, 'pipe', 'tp', 'ctx')
- span_order: int32 [8], replicated, may hold values from 0 to 7, each once
- fwd_docs: int32 [4, 256], replicated, may hold values from 0 to 3, never falling along the last dimension, each value on 1 to 128 neighbouring positions
- back_docs: int32 [4, 256], replicated, may hold values from 0 to 3, never falling along the last dimension, each value on 1 to 128 neighbouring positions
Outputs:
- fwd_out: bfloat16 [4, 256, 16384], P('pipe', 'ctx', 'tp')
- back_out: bfloat16 [4, 256, 16384], P('pipe', 'ctx', 'tp')
The draws below stay inside these ranges and needn't reach their ends.
Inputs may be any that keep to these rules, and one draw needn't show every extreme that they name: Each span number appears once; device i of ctx stores spans span_order[4 * i] to span_order[4 i + 3]. `fwd_docs`: ids never fall along positions; each document covers 1 to 128 positions, one exactly 128. `back_docs`: ids never fall along positions; each document covers 1 to 128 positions, one exactly 128.
All inputs are finite; a program needn't handle non-finite values.
Results may differ from the reference program's by a relative error of at most 0.014.
The reference program's roundings to bfloat16 on the way count: a program that leaves them out, or rounds other values in their place, can miss the bound.
Values may be sent and summed in bfloat16 or wider, within the bound.
A program may use at most 384 MiB of HBM per device.

```python
import math
import jax
import jax.numpy as jnp
import numpy as np
from jax import lax

D = 16384
HD = 128
QH = 8
SPANS = 4
SPAN = 32
TICKS = 3
SEQ = 256
N_PIPE = 4
N_CTX = 2


def draw_layer_weights(key, part):
    normals = jax.random.normal(key, (2, N_PIPE, D, 2 * QH * HD + 2 * HD), jnp.float32)
    qkv_cols = QH * HD + 2 * HD
    projection = normals[..., :qkv_cols] * D ** (-0.5)
    out_cols = normals[..., qkv_cols:] * (QH * HD) ** (-0.5)
    return jnp.concatenate([projection, out_cols], axis=-1).astype(jnp.bfloat16)


def block_levels(stream_key, extent, shards, smallest, largest):
    level, own = 1.0, jax.random.fold_in(stream_key, 6)
    for position, shards_of in shards:
        draws = jnp.exp(jax.random.uniform(jax.random.fold_in(own, position), (shards_of,), jnp.float32, smallest / len(shards), largest / len(shards)))
        level = level * jnp.repeat(draws, extent[position] // shards_of).reshape([-1 if axis == position else 1 for axis in range(len(extent))])
    return level


def length_profile(amount, total, reach, lean):
    portions = [(1 << 20) // math.isqrt(grade ** lean) + 1 for grade in range(2, amount + 1)]
    spare, counts = total - reach - (amount - 1), [1] * (amount - 1)
    while spare > 0:
        candidates = [i for i in range(amount - 1) if counts[i] < reach]
        whole, budget = sum([portions[i] for i in candidates]), spare
        for i in candidates:
            more = min(reach - counts[i], max(1, budget * portions[i] // whole), spare)
            counts[i] = counts[i] + more
            spare = spare - more
    return np.array([reach] + counts)


def ragged(key, count, total, reach, lean):
    if count == 2:
        one = jax.random.randint(key, (), max(1, total - reach), min(reach, total - 1) + 1)
        return jnp.stack([one, total - one])
    lengths = jnp.asarray(length_profile(count, total, reach, lean), jnp.int32)
    pairs = (count - 1) // 2
    source_of, taker = lengths[1:1 + 2 * pairs:2], lengths[2:2 + 2 * pairs:2]
    room = jnp.minimum(source_of - 1, reach - taker)
    shifted = jax.random.randint(jax.random.fold_in(key, 1), (pairs,), 0, 1 << 20) % (room + 1)
    lengths = lengths.at[1:1 + 2 * pairs:2].set(source_of - shifted).at[2:2 + 2 * pairs:2].set(taker + shifted)
    return lengths[jax.random.permutation(jax.random.fold_in(key, 2), count)]


def scatter_about(rng, shape, spread, most, cuts=(), kind=jnp.bfloat16):
    loudness = block_levels(rng, shape, cuts, -0.22, 0.18) if cuts else 1.0
    values = jax.random.normal(rng, shape, jnp.float32) * spread * loudness
    return jnp.minimum(jnp.maximum(values, -most), most).astype(kind)


def setup_inputs(seed: int = 0) -> dict:
    arg_keys = jax.random.split(jax.random.key(seed), 8)
    fwd_acts = scatter_about(arg_keys[0], (N_PIPE, SEQ, D), 1.0, 6.0, ((0, 4), (1, 2), (2, 4)))
    back_grads = scatter_about(arg_keys[1], (N_PIPE, SEQ, D), 1.0, 6.0, ((0, 4), (1, 2), (2, 4)))
    stashed = scatter_about(arg_keys[2], (N_PIPE, TICKS, SEQ, D), 1.0, 6.0, ((0, 4), (2, 2), (3, 4)))
    layer_weights = draw_layer_weights(jax.random.fold_in(arg_keys[7], 71), 0)
    span_order = jax.random.permutation(arg_keys[4], SPANS * N_CTX).astype(jnp.int32)
    fwd_docs = jax.vmap(lambda own: jnp.searchsorted(jnp.cumsum(ragged(own, 4, SEQ, SEQ // 2, 1)), jnp.arange(SEQ), side="right"))(jax.random.split(arg_keys[5], N_PIPE)).reshape((N_PIPE, SEQ)).astype(jnp.int32)
    back_docs = jax.vmap(lambda own: jnp.searchsorted(jnp.cumsum(ragged(own, 4, SEQ, SEQ // 2, 1)), jnp.arange(SEQ), side="right"))(jax.random.split(arg_keys[6], N_PIPE)).reshape((N_PIPE, SEQ)).astype(jnp.int32)
    return {"fwd_acts": fwd_acts, "back_grads": back_grads, "stashed": stashed, "layer_weights": layer_weights, "span_order": span_order, "fwd_docs": fwd_docs, "back_docs": back_docs}


EPSILON = 1e-05

def visible(query_pos, query_doc, key_pos, key_doc):
    return (key_pos[None, :] <= query_pos[:, None]) & (key_doc[None, :] == query_doc[:, None])

def softmax_rows(scores, visible_mask):
    masked = jnp.where(visible_mask, scores, -jnp.inf)
    row_max = lax.optimization_barrier(jnp.max(masked, axis=-1, keepdims=True))
    exponent = jnp.where(visible_mask, jnp.exp(masked - row_max), 0.0)
    return exponent / lax.optimization_barrier(jnp.sum(exponent, axis=-1, keepdims=True))

def project(hidden, weight):
    qkv_cols = QH * HD + 2 * HD
    hidden_f = hidden.astype(jnp.float32)
    inv_rms = lax.rsqrt(lax.optimization_barrier(jnp.mean(hidden_f * hidden_f, axis=1)) + EPSILON)
    merged = jnp.dot(hidden, weight[:, :qkv_cols], preferred_element_type=jnp.float32)
    qkv = (inv_rms[:, None] * merged).astype(jnp.bfloat16)
    return (inv_rms, merged, qkv)

def split_heads(qkv):
    rows = qkv.shape[0]
    queries = qkv[:, :QH * HD].reshape(rows, QH, HD).astype(jnp.float32)
    keys_all = qkv[:, QH * HD:QH * HD + HD].astype(jnp.float32)
    values_all = qkv[:, QH * HD + HD:QH * HD + 2 * HD].astype(jnp.float32)
    return (queries, keys_all, values_all)

def forward_layer(hidden, weight, visible_mask):
    qkv_cols = QH * HD + 2 * HD
    score_scale = HD ** (-0.5)
    rows = hidden.shape[0]
    inv_rms, merged, qkv = project(hidden, weight)
    queries, keys_all, values_all = split_heads(qkv)
    scores = jnp.einsum('qhc,kc->hqk', queries, keys_all) * score_scale
    attn_probs = softmax_rows(scores, visible_mask[None]).astype(jnp.bfloat16)
    attended = jnp.einsum('hqk,kc->qhc', attn_probs.astype(jnp.float32), values_all)
    attended = attended.reshape(rows, QH * HD).astype(jnp.bfloat16)
    update = jnp.dot(attended, weight[:, qkv_cols:].T, preferred_element_type=jnp.float32)
    return (hidden.astype(jnp.float32) + update).astype(jnp.bfloat16)

def backward_layer(stash_point, incoming, weight, visible_mask):
    qkv_cols = QH * HD + 2 * HD
    score_scale = HD ** (-0.5)
    rows = stash_point.shape[0]
    model_width = stash_point.shape[1]
    inv_rms, merged, qkv = project(stash_point, weight)
    queries, keys_all, values_all = split_heads(qkv)
    out_grad = jnp.dot(incoming, weight[:, qkv_cols:], preferred_element_type=jnp.float32).astype(jnp.bfloat16)
    out_heads = out_grad.reshape(rows, QH, HD).astype(jnp.float32)
    scores = jnp.einsum('qhc,kc->hqk', queries, keys_all) * score_scale
    attn_probs = softmax_rows(scores, visible_mask[None])
    probs_low = attn_probs.astype(jnp.bfloat16).astype(jnp.float32)
    grad_prob = jnp.einsum('qhc,kc->hqk', out_heads, values_all)
    delta_row = lax.optimization_barrier(jnp.sum(attn_probs * grad_prob, axis=-1, keepdims=True))
    grad_score = (attn_probs * (grad_prob - delta_row) * score_scale).astype(jnp.bfloat16).astype(jnp.float32)
    grad_query = jnp.einsum('hqk,kc->qhc', grad_score, keys_all).reshape(rows, QH * HD)
    grad_key = jnp.einsum('hqk,qhc->kc', grad_score, queries)
    grad_value = jnp.einsum('hqk,qhc->kc', probs_low, out_heads)
    grad_qkv = jnp.concatenate([grad_query, grad_key, grad_value], axis=1).astype(jnp.bfloat16)
    grad_scale = lax.optimization_barrier(jnp.sum(grad_qkv.astype(jnp.float32) * merged, axis=1))
    back_term = jnp.dot(grad_qkv, weight[:, :qkv_cols].T, preferred_element_type=jnp.float32)
    result = incoming.astype(jnp.float32) + inv_rms[:, None] * back_term
    result = result - (inv_rms ** 3 * grad_scale / model_width)[:, None] * stash_point.astype(jnp.float32)
    return result.astype(jnp.bfloat16)

def reference(fwd_acts, back_grads, stashed, layer_weights, span_order, fwd_docs, back_docs):
    sections = N_PIPE
    offsets = jnp.arange(SPAN, dtype=jnp.int32)
    positions = (span_order[:, None].astype(jnp.int32) * SPAN + offsets[None, :]).reshape(-1)
    fwd_results = []
    for slot_index in range(sections):
        documents = fwd_docs[slot_index].reshape(-1, SPAN)[span_order].reshape(-1)
        visible_mask = visible(positions, documents, positions, documents)
        hidden = fwd_acts[slot_index]
        for tick_index in range(TICKS):
            layer_index = slot_index + tick_index
            weight = layer_weights[layer_index // sections, layer_index % sections]
            hidden = forward_layer(hidden, weight, visible_mask)
        fwd_results.append(hidden)
    back_results = []
    for slot_index in range(sections):
        documents = back_docs[slot_index].reshape(-1, SPAN)[span_order].reshape(-1)
        visible_mask = visible(positions, documents, positions, documents)
        incoming = back_grads[slot_index]
        for tick_index in range(TICKS):
            layer_index = sections + slot_index - tick_index
            weight = layer_weights[layer_index // sections, layer_index % sections]
            stash_point = stashed[(slot_index - tick_index) % sections, tick_index]
            incoming = backward_layer(stash_point, incoming, weight, visible_mask)
        back_results.append(incoming)
    fwd_out = jnp.stack([fwd_results[(place - TICKS) % sections] for place in range(sections)])
    back_out = jnp.stack([back_results[(place + TICKS) % sections] for place in range(sections)])
    return (fwd_out, back_out)
```

```python
import functools

import jax
import jax.numpy as jnp
from jax import lax
from jax.experimental import pallas as pl
from jax.experimental.pallas import tpu as pltpu
from jax.sharding import PartitionSpec as P

HD = 128
QH = 8
SPANS = 4


EPSILON = 1e-05


def from_behind(block, axis, distance):
    devices = range(lax.axis_size(axis))
    route = [((i - distance) % len(devices), i) for i in devices]
    return lax.ppermute(block, axis, route)


def visible(query_pos, query_doc, key_pos, key_doc):
    return (key_pos[None, :] <= query_pos[:, None]) & (key_doc[None, :] == query_doc[:, None])


def softmax_rows(scores, visible_mask):
    masked = jnp.where(visible_mask, scores, -jnp.inf)
    row_max = jnp.max(masked, axis=-1, keepdims=True)
    exponent = jnp.where(visible_mask, jnp.exp(masked - row_max), 0.0)
    return exponent / jnp.sum(exponent, axis=-1, keepdims=True)


def seq_documents(docs_table, slot_index, span_order, span_len):
    docs_row = lax.dynamic_index_in_dim(docs_table, slot_index, 0, keepdims=False)
    return docs_row.reshape(-1, span_len)[span_order].reshape(-1)


def forward_layer(hidden, weight, positions, documents, ctx_rank, model_width):
    row_count = hidden.shape[0]
    qkv_cols = QH * HD + 2 * HD
    score_scale = HD ** (-0.5)
    hidden_f = hidden.astype(jnp.float32)
    partial_m = jnp.dot(hidden, weight[:, :qkv_cols], preferred_element_type=jnp.float32)
    partial_sq = jnp.sum(hidden_f * hidden_f, axis=1)
    merged, squares = lax.psum((partial_m, partial_sq), "tp")
    inv_rms = lax.rsqrt(squares / model_width + EPSILON)
    qkv = (inv_rms[:, None] * merged).astype(jnp.bfloat16)
    queries = qkv[:, : QH * HD].reshape(row_count, QH, HD)
    keys_own = qkv[:, QH * HD : QH * HD + HD]
    values_own = qkv[:, QH * HD + HD : qkv_cols]
    keys_all, values_all = (
        lax.all_gather(keys_own, "ctx", axis=0, tiled=True),
        lax.all_gather(values_own, "ctx", axis=0, tiled=True),
    )
    own_pos = lax.dynamic_slice_in_dim(positions, ctx_rank * row_count, row_count)
    own_doc = lax.dynamic_slice_in_dim(documents, ctx_rank * row_count, row_count)
    visible_mask = visible(own_pos, own_doc, positions, documents)
    scores = (
        jnp.einsum("qhc,kc->hqk", queries, keys_all, preferred_element_type=jnp.float32)
        * score_scale
    )
    attn_probs = softmax_rows(scores, visible_mask[None]).astype(jnp.bfloat16)
    attended = jnp.einsum("hqk,kc->qhc", attn_probs, values_all, preferred_element_type=jnp.float32)
    attended = attended.reshape(row_count, QH * HD).astype(jnp.bfloat16)
    update = jnp.einsum(
        "rc,dc->rd", attended, weight[:, qkv_cols:], preferred_element_type=jnp.float32
    )
    return (hidden_f + update).astype(jnp.bfloat16)


def backward_layer(stash_point, incoming, weight, positions, documents, ctx_rank, model_width):
    row_count = stash_point.shape[0]
    qkv_cols = QH * HD + 2 * HD
    score_scale = HD ** (-0.5)
    stash_f = stash_point.astype(jnp.float32)
    partial_m = jnp.dot(stash_point, weight[:, :qkv_cols], preferred_element_type=jnp.float32)
    partial_sq = jnp.sum(stash_f * stash_f, axis=1)
    partial_out = jnp.dot(incoming, weight[:, qkv_cols:], preferred_element_type=jnp.float32)
    merged, squares, out_sum = lax.psum((partial_m, partial_sq, partial_out), "tp")
    inv_rms = lax.rsqrt(squares / model_width + EPSILON)
    qkv = (inv_rms[:, None] * merged).astype(jnp.bfloat16)
    out_grad = out_sum.astype(jnp.bfloat16)
    query_flat = qkv[:, : QH * HD]
    keys_own = qkv[:, QH * HD : QH * HD + HD]
    values_own = qkv[:, QH * HD + HD : qkv_cols]
    keys_all, values_all = (
        lax.all_gather(keys_own, "ctx", axis=0, tiled=True),
        lax.all_gather(values_own, "ctx", axis=0, tiled=True),
    )
    row_start = ctx_rank * row_count
    query_heads = query_flat.reshape(row_count, QH, HD)
    out_heads = out_grad.reshape(row_count, QH, HD)
    own_pos = lax.dynamic_slice_in_dim(positions, row_start, row_count)
    own_doc = lax.dynamic_slice_in_dim(documents, row_start, row_count)
    visible_mask = visible(own_pos, own_doc, positions, documents)
    scores = (
        jnp.einsum("qhc,kc->hqk", query_heads, keys_all, preferred_element_type=jnp.float32)
        * score_scale
    )
    attn_probs = softmax_rows(scores, visible_mask[None])
    probs_low = attn_probs.astype(jnp.bfloat16)
    grad_prob = jnp.einsum("qhc,kc->hqk", out_heads, values_all, preferred_element_type=jnp.float32)
    delta_row = jnp.sum(attn_probs * grad_prob, axis=-1, keepdims=True)
    grad_score = (attn_probs * (grad_prob - delta_row) * score_scale).astype(jnp.bfloat16)
    grad_query = jnp.einsum("hqk,kc->qhc", grad_score, keys_all, preferred_element_type=jnp.float32)
    grad_query = grad_query.reshape(row_count, QH * HD)
    key_terms = jnp.einsum(
        "hqk,qhc->kc", grad_score, query_heads, preferred_element_type=jnp.float32
    )
    value_terms = jnp.einsum(
        "hqk,qhc->kc", probs_low, out_heads, preferred_element_type=jnp.float32
    )
    grad_key, grad_value = (
        lax.psum_scatter(key_terms, "ctx", scatter_dimension=0, tiled=True),
        lax.psum_scatter(value_terms, "ctx", scatter_dimension=0, tiled=True),
    )
    grad_qkv = jnp.concatenate([grad_query, grad_key, grad_value], axis=1).astype(jnp.bfloat16)
    grad_scale = jnp.sum(grad_qkv.astype(jnp.float32) * merged, axis=1)
    back_term = jnp.einsum(
        "rc,dc->rd", grad_qkv, weight[:, :qkv_cols], preferred_element_type=jnp.float32
    )
    result = incoming.astype(jnp.float32) + inv_rms[:, None] * back_term
    result = result - (inv_rms**3 * grad_scale / model_width)[:, None] * stash_f
    return result.astype(jnp.bfloat16)


def plain_body(fwd_acts, back_grads, stashed, layer_weights, span_order, fwd_docs, back_docs):
    sections = lax.axis_size("pipe")
    section_index = lax.axis_index("pipe")
    ctx_rank = lax.axis_index("ctx")
    row_count = fwd_acts.shape[1]
    span_len = row_count // SPANS
    model_width = fwd_acts.shape[2] * lax.axis_size("tp")
    tick_count = stashed.shape[1]
    offsets = jnp.arange(span_len, dtype=jnp.int32)
    positions = (span_order[:, None] * span_len + offsets[None, :]).reshape(-1)
    gathered = lax.all_gather(layer_weights, "ctx", axis=3, tiled=True)[:, 0]
    fwd_state = fwd_acts[0]
    back_state = back_grads[0]
    for tick_index in range(tick_count):
        fwd_slot = (section_index - tick_index) % sections
        fwd_half = jnp.where(section_index < tick_index, 1, 0)
        fwd_weight = lax.dynamic_index_in_dim(gathered, fwd_half, 0, keepdims=False)
        fwd_documents = seq_documents(fwd_docs, fwd_slot, span_order, span_len)
        fwd_state = forward_layer(
            fwd_state, fwd_weight, positions, fwd_documents, ctx_rank, model_width
        )
        fwd_state = from_behind(fwd_state, "pipe", 1)
        back_slot = (section_index + tick_index) % sections
        back_half = jnp.where(section_index + tick_index < sections, 1, 0)
        back_weight = lax.dynamic_index_in_dim(gathered, back_half, 0, keepdims=False)
        back_documents = seq_documents(back_docs, back_slot, span_order, span_len)
        back_state = backward_layer(
            stashed[0, tick_index],
            back_state,
            back_weight,
            positions,
            back_documents,
            ctx_rank,
            model_width,
        )
        back_state = from_behind(back_state, "pipe", -1)
    return (fwd_state[None], back_state[None])


QKV = QH * HD + 2 * HD
OC = QH * HD
WIDE = 256
PARTIAL = jnp.float32
MESH = pl.DeviceIdType.MESH
TRANS_B = (((1,), (1,)), ((), ()))
TRANS_A = (((0,), (0,)), ((), ()))


def dot_nt(a, b):
    return lax.dot_general(a, b, TRANS_B, preferred_element_type=jnp.float32)


def dot_tn(a, b):
    return lax.dot_general(a, b, TRANS_A, preferred_element_type=jnp.float32)


def dot_nn(a, b):
    return jnp.dot(a, b, preferred_element_type=jnp.float32)


class Place:
    def __init__(self, send_sem, recv_sem):
        self.p, self.c, self.t = (lax.axis_index(a) for a in ("pipe", "ctx", "tp"))
        self.n = lax.axis_size("tp")
        self.send_sem, self.recv_sem = send_sem, recv_sem

    def to(self, d):
        return lax.rem(self.t + d, self.n)

    def source(self, d):
        return lax.rem(self.t + self.n - d, self.n)

    def copy(self, src, dst, sem, c, t):
        return pltpu.make_async_remote_copy(
            src_ref=src,
            dst_ref=dst,
            send_sem=self.send_sem.at[sem],
            recv_sem=self.recv_sem.at[sem],
            device_id=(self.p, c, t),
            device_id_type=MESH,
        )

    def partner(self, src, dst, sem):
        return self.copy(src, dst, sem, 1 - self.c, self.t)

    def barrier(self):
        sem = pltpu.get_barrier_semaphore()
        for d in range(self.n):
            for other in (0, 1):
                if d == 0 and other == 0:
                    continue
                c = self.c if other == 0 else 1 - self.c
                pl.semaphore_signal(sem, inc=1, device_id=(self.p, c, self.to(d)), device_id_type=MESH)
        pl.semaphore_wait(sem, 2 * self.n - 1)


def row_squares(full, sq):
    @pl.loop(0, full.shape[0] // 32)
    def _(i):
        rows = pl.ds(pl.multiple_of(i * 32, 32), 32)
        x = full[rows, :].astype(jnp.float32)
        sq[rows, :] = jnp.broadcast_to(jnp.sum(x * x, axis=1, keepdims=True), (32, HD))


def project_cols(full, w, first, count, out):
    @pl.loop(0, count // WIDE)
    def _(i):
        at = pl.multiple_of(i * WIDE, WIDE)
        res = dot_nn(full[...], w[:, pl.ds(pl.multiple_of(first + at, HD), WIDE)])
        out[:, pl.ds(at, WIDE)] = res.astype(out.dtype)


def scatter_start(pc, part, landing, cols, base, rows):
    copies = []
    for d in range(1, pc.n):
        to = pc.to(d)
        mine = pl.ds(pl.multiple_of(to * rows, rows), rows)
        cp = pc.copy(part.at[mine, pl.ds(0, cols)], landing.at[d - 1, :, pl.ds(0, cols)], base + d, pc.c, to)
        cp.start()
        copies.append(cp)
    return copies


def scatter_sum(pc, copies, part, landing, cols, rows):
    total = part[pl.ds(pl.multiple_of(pc.t * rows, rows), rows), pl.ds(0, cols)].astype(jnp.float32)
    for d, cp in enumerate(copies):
        cp.wait_recv()
        total = total + landing[d, :, pl.ds(0, cols)].astype(jnp.float32)
    for cp in copies:
        cp.wait_send()
    return total


def gather_start(pc, whole, base, rows, c, first=1):
    mine = pl.ds(pl.multiple_of(pc.t * rows, rows), rows)
    copies = []
    for d in range(first, pc.n):
        cp = pc.copy(whole.at[mine], whole.at[mine], base + d, c, pc.to(d))
        cp.start()
        copies.append(cp)
    return copies


def gather_wait(pc, whole, base, rows, first=1):
    for d in range(first, pc.n):
        there = pl.ds(pl.multiple_of(pc.source(d) * rows, rows), rows)
        pc.copy(whole.at[there], whole.at[there], base + d, pc.c, pc.source(d)).wait_recv()


def probabilities(q, k, seen):
    scores = dot_nt(q, k) * (HD ** (-0.5))
    masked = jnp.where(seen, scores, -jnp.inf)
    top = jnp.max(masked, axis=-1, keepdims=True)
    e = jnp.where(seen, jnp.exp(masked - top), 0.0)
    return e / jnp.sum(e, axis=-1, keepdims=True)


def qkv_rows(pc, width, full, w, part, landing, sq, sq_in, kv, m_ref, q_ref, base, rows):
    row_squares(full, sq)
    sq_copies = scatter_start(pc, sq, sq_in, HD, base, rows)
    project_cols(full, w, 0, QKV, part)
    copies = scatter_start(pc, part, landing, QKV, base + 4, rows)
    squares = scatter_sum(pc, sq_copies, sq, sq_in, HD, rows)
    m = scatter_sum(pc, copies, part, landing, QKV, rows)
    r = lax.rsqrt(squares / width + EPSILON)
    qkv = (r[:, :1] * m).astype(jnp.bfloat16)
    if m_ref is not None:
        m_ref[...] = m
    q_ref[...] = qkv[:, :OC]
    mine = pl.ds(pl.multiple_of(pc.t * rows, rows), rows)
    kv[mine, :] = qkv[:, OC:]
    kv_copies = gather_start(pc, kv, base + 8, rows, 0)
    gather_wait(pc, kv, base + 8, rows)
    for cp in kv_copies:
        cp.wait_send()
    return r


PIECES = 4


def hand_over(pc, stage, landed, out, base, make):
    span = out.shape[1] // PIECES
    copies = []
    for piece in range(PIECES):
        make(piece, span)
        cols = pl.ds(piece * span, span)
        cp = pc.partner(stage.at[:, cols], landed.at[:, cols], base + piece)
        cp.start()
        copies.append(cp)
    for cp in copies:
        cp.wait_send()


def take_over(pc, stage, landed, out, base):
    span = out.shape[1] // PIECES
    for piece in range(PIECES):
        cols = pl.ds(piece * span, span)
        pc.partner(stage.at[:, cols], landed.at[:, cols], base + piece).wait_recv()
        out[:, cols] = landed[:, cols]


def fetch_weight(pc, w_hbm, w, half, sem):
    local = pltpu.make_async_copy(w_hbm.at[half], w.at[:, pl.ds(0, w_hbm.shape[2])], sem)
    local.start()
    return local


def values_weight(pc, w_hbm, w, half, sem):
    return pc.partner(w_hbm.at[half, :, pl.ds(0, HD)], w.at[:, pl.ds(QKV - HD, HD)], sem)


def forward_kernel(tick, width, seen_ref, h_ref, w_hbm, out_ref, w, full, part, landing, sq, sq_in,
                   kv, q_ref, o_all, stage, landed, local_sem, send_sem, recv_sem):
    pc = Place(send_sem, recv_sem)
    own = h_ref.shape[0]
    rows = 2 * own // pc.n
    sections = lax.axis_size("pipe")
    half = (sections + tick - 1 - pc.p) // sections
    local = fetch_weight(pc, w_hbm, w, half, local_sem)
    pc.barrier()
    own_rows = pl.ds(pl.multiple_of(pc.c * own, own), own)
    hop = pc.partner(h_ref, full.at[own_rows], 0)
    hop.start()
    extra = values_weight(pc, w_hbm, w, half, 1)

    @pl.when(pc.c == 1)
    def _():
        extra.start()

    full[own_rows, :] = h_ref[...]
    other_rows = pl.ds(pl.multiple_of((1 - pc.c) * own, own), own)
    pc.partner(h_ref, full.at[other_rows], 0).wait_recv()
    local.wait()

    @pl.when(pc.c == 0)
    def _():
        extra.wait_recv()
        qkv_rows(pc, width, full, w, part, landing, sq, sq_in, kv, None, q_ref, 8, rows)
        seen = seen_ref[...] > 0.0
        mine = pl.ds(pl.multiple_of(pc.t * rows, rows), rows)
        for h in range(QH):
            cols = pl.ds(h * HD, HD)
            p = probabilities(q_ref[:, cols], kv[:, pl.ds(0, HD)], seen).astype(jnp.bfloat16)
            o_all[mine, cols] = dot_nn(p, kv[:, pl.ds(HD, HD)]).astype(jnp.bfloat16)
        copies = gather_start(pc, o_all, 20, rows, 1, first=0)
        for cp in copies:
            cp.wait_send()
        take_over(pc, stage, landed, out_ref, 24)

    @pl.when(pc.c == 1)
    def _():
        extra.wait_send()
        gather_wait(pc, o_all, 20, rows, first=0)

        def make(piece, span):
            @pl.loop(0, span // WIDE)
            def _(i):
                at = pl.multiple_of(piece * span + i * WIDE, WIDE)
                cols = pl.ds(at, WIDE)
                update = dot_nt(o_all[...], w[cols, pl.ds(HD, OC)])
                res = (full[:, cols].astype(jnp.float32) + update).astype(jnp.bfloat16)
                stage[:, cols] = res[:own]
                out_ref[:, cols] = res[own:]

        hand_over(pc, stage, landed, out_ref, 24, make)

    hop.wait_send()


def backward_kernel(tick, width, seen_ref, u_ref, g_ref, w_hbm, out_ref, w, full, gfull, part, landing,
                    sq, sq_in, kv, q_ref, m_ref, go_ref, dkv, dkv_in, e_all, rc, stage, landed,
                    local_sem, send_sem, recv_sem):
    pc = Place(send_sem, recv_sem)
    own = u_ref.shape[0]
    rows = 2 * own // pc.n
    sections = lax.axis_size("pipe")
    half = (2 * sections - 1 - pc.p - tick) // sections
    local = fetch_weight(pc, w_hbm, w, half, local_sem)
    pc.barrier()
    own_rows = pl.ds(pl.multiple_of(pc.c * own, own), own)
    other_rows = pl.ds(pl.multiple_of((1 - pc.c) * own, own), own)
    extra = values_weight(pc, w_hbm, w, half, 1)
    uhop = pc.partner(u_ref, full.at[own_rows], 0)
    ghop = pc.partner(g_ref, gfull.at[own_rows], 2)

    @pl.when(pc.c == 1)
    def _():
        uhop.start()
        extra.start()

    ghop.start()
    gfull[own_rows, :] = g_ref[...]
    local.wait()

    @pl.when(pc.c == 0)
    def _():
        full[own_rows, :] = u_ref[...]
        pc.partner(u_ref, full.at[other_rows], 0).wait_recv()
        extra.wait_recv()
        r = qkv_rows(pc, width, full, w, part, landing, sq, sq_in, kv, m_ref, q_ref, 8, rows)
        pc.partner(go_ref, go_ref, 3).wait_recv()
        seen = seen_ref[...] > 0.0
        mine = pl.ds(pl.multiple_of(pc.t * rows, rows), rows)
        k, v = kv[:, pl.ds(0, HD)], kv[:, pl.ds(HD, HD)]
        dr = jnp.zeros((rows, 1), jnp.float32)
        dk = jnp.zeros((2 * own, HD), jnp.float32)
        dv = jnp.zeros((2 * own, HD), jnp.float32)
        for h in range(QH):
            cols = pl.ds(h * HD, HD)
            q, go = q_ref[:, cols], go_ref[:, cols]
            p = probabilities(q, k, seen)
            dp = dot_nt(go, v)
            delta = jnp.sum(p * dp, axis=-1, keepdims=True)
            ds = (p * (dp - delta) * (HD ** (-0.5))).astype(jnp.bfloat16)
            dq = dot_nn(ds, k).astype(jnp.bfloat16)
            e_all[mine, cols] = dq
            dr = dr + jnp.sum(dq.astype(jnp.float32) * m_ref[:, cols], axis=1, keepdims=True)
            dk = dk + dot_tn(ds, q)
            dv = dv + dot_tn(p.astype(jnp.bfloat16), go)
        dkv[:, pl.ds(0, HD)] = dk
        dkv[:, pl.ds(HD, HD)] = dv
        copies = scatter_start(pc, dkv, dkv_in, 2 * HD, 24, rows)
        last = scatter_sum(pc, copies, dkv, dkv_in, 2 * HD, rows).astype(jnp.bfloat16)
        e_all[mine, pl.ds(OC, 2 * HD)] = last
        dr = dr + jnp.sum(last.astype(jnp.float32) * m_ref[:, pl.ds(OC, 2 * HD)], axis=1, keepdims=True)
        rc[mine, pl.ds(0, HD)] = r
        rc[mine, pl.ds(HD, HD)] = r * r * r * dr / width
        copies = gather_start(pc, e_all, 28, rows, 0) + gather_start(pc, rc, 32, rows, 0)
        gather_wait(pc, e_all, 28, rows)
        gather_wait(pc, rc, 32, rows)
        for cp in copies:
            cp.wait_send()
        pc.partner(g_ref, gfull.at[other_rows], 2).wait_recv()

        def make(piece, span):
            @pl.loop(0, span // WIDE)
            def _(i):
                at = pl.multiple_of(piece * span + i * WIDE, WIDE)
                cols = pl.ds(at, WIDE)
                back = dot_nt(e_all[...], w[cols, :])
                res = gfull[:, cols].astype(jnp.float32) + rc[:, pl.ds(0, 1)] * back
                res = res - rc[:, pl.ds(HD, 1)] * full[:, cols].astype(jnp.float32)
                res = res.astype(jnp.bfloat16)
                out_ref[:, cols] = res[:own]
                stage[:, cols] = res[own:]

        hand_over(pc, stage, landed, out_ref, 36, make)

    @pl.when(pc.c == 1)
    def _():
        pc.partner(g_ref, gfull.at[other_rows], 2).wait_recv()
        project_cols(gfull, w, HD, OC, part)
        copies = scatter_start(pc, part, landing, OC, 20, rows)
        go_ref[...] = scatter_sum(pc, copies, part, landing, OC, rows).astype(jnp.bfloat16)
        give = pc.partner(go_ref, go_ref, 3)
        give.start()
        give.wait_send()
        uhop.wait_send()
        extra.wait_send()
        take_over(pc, stage, landed, out_ref, 36)

    ghop.wait_send()


def call(kernel, collective_id, operands, specs, like, scratch, flops):
    return pl.pallas_call(
        kernel,
        out_shape=jax.ShapeDtypeStruct(like.shape, like.dtype),
        in_specs=specs,
        out_specs=pl.BlockSpec(memory_space=pltpu.VMEM),
        scratch_shapes=scratch + [pltpu.SemaphoreType.DMA, pltpu.SemaphoreType.DMA((40,)), pltpu.SemaphoreType.DMA((40,))],
        compiler_params=pltpu.CompilerParams(
            collective_id=collective_id, has_side_effects=True, vmem_limit_bytes=48 * 2**20
        ),
        cost_estimate=pl.CostEstimate(flops=flops, bytes_accessed=12 * 2**20, transcendentals=0),
    )(*operands)


def fused_body(fwd_acts, back_grads, stashed, layer_weights, span_order, fwd_docs, back_docs):
    sections, n = lax.axis_size("pipe"), lax.axis_size("tp")
    p, t = lax.axis_index("pipe"), lax.axis_index("tp")
    own, model = fwd_acts.shape[1:]
    seq = 2 * own
    rows = seq // n
    span = own // SPANS
    width = model * n
    ticks = stashed.shape[1]
    offsets = jnp.arange(span, dtype=jnp.int32)
    positions = (span_order[:, None] * span + offsets[None, :]).reshape(-1)
    weights = layer_weights[:, 0]
    bf, f32 = jnp.bfloat16, jnp.float32
    vm = pltpu.VMEM
    shared = [
        vm((seq, QKV), PARTIAL), vm((n - 1, rows, QKV), PARTIAL), vm((seq, HD), f32),
        vm((n - 1, rows, HD), f32), vm((seq, 2 * HD), bf), vm((rows, OC), bf),
    ]
    edge = [vm((own, model), bf), vm((own, model), bf)]
    fwd_scratch = [vm((model, QKV), bf), vm((seq, model), bf)] + shared + [vm((seq, OC), bf)] + edge
    back_scratch = [vm((model, QKV), bf), vm((seq, model), bf), vm((seq, model), bf)] + shared + [
        vm((rows, QKV), f32), vm((rows, OC), bf), vm((seq, 2 * HD), f32), vm((n - 1, rows, 2 * HD), f32),
        vm((seq, QKV), bf), vm((seq, 2 * HD), f32)] + edge
    in_vmem = pl.BlockSpec(memory_space=pltpu.VMEM)
    anywhere = pl.BlockSpec(memory_space=pl.ANY)

    def seen(docs, slot):
        documents = seq_documents(docs, slot, span_order, span)
        my_pos = lax.dynamic_slice_in_dim(positions, t * rows, rows)
        my_doc = lax.dynamic_slice_in_dim(documents, t * rows, rows)
        return visible(my_pos, my_doc, positions, documents).astype(f32)

    fwd, back = fwd_acts[0], back_grads[0]
    for tick in range(ticks):
        fwd_seen = seen(fwd_docs, (p - tick) % sections)
        fwd = call(functools.partial(forward_kernel, tick, width), tick, (fwd_seen, fwd, weights),
                   [in_vmem, in_vmem, anywhere], fwd, fwd_scratch, 3 * 10**10)
        fwd = from_behind(fwd, "pipe", 1)
        back_seen = seen(back_docs, (p + tick) % sections)
        back = call(functools.partial(backward_kernel, tick, width), ticks + tick,
                    (back_seen, stashed[0, tick], back, weights),
                    [in_vmem, in_vmem, in_vmem, anywhere], back, back_scratch, 3 * 10**10)
        back = from_behind(back, "pipe", -1)
    return (fwd[None], back[None])


def solution(mesh):
    return jax.shard_map(
        fused_body if mesh.shape["tp"] <= 4 else plain_body,
        mesh=mesh,
        in_specs=(
            P("pipe", "ctx", "tp"),
            P("pipe", "ctx", "tp"),
            P("pipe", None, "ctx", "tp"),
            P(None, "pipe", "tp", "ctx"),
            P(),
            P(),
            P(),
        ),
        out_specs=(P("pipe", "ctx", "tp"), P("pipe", "ctx", "tp")),
        check_vma=False,
    )
```

```python
import functools

import jax
import jax.numpy as jnp
from jax import lax
from jax.experimental import pallas as pl
from jax.experimental.pallas import tpu as pltpu
from jax.sharding import PartitionSpec as P

HD = 128
QH = 8
SPANS = 4


EPSILON = 1e-05


def from_behind(block, axis, distance):
    devices = range(lax.axis_size(axis))
    route = [((i - distance) % len(devices), i) for i in devices]
    return lax.ppermute(block, axis, route)


def visible(query_pos, query_doc, key_pos, key_doc):
    return (key_pos[None, :] <= query_pos[:, None]) & (key_doc[None, :] == query_doc[:, None])


def softmax_rows(scores, visible_mask):
    masked = jnp.where(visible_mask, scores, -jnp.inf)
    row_max = jnp.max(masked, axis=-1, keepdims=True)
    exponent = jnp.where(visible_mask, jnp.exp(masked - row_max), 0.0)
    return exponent / jnp.sum(exponent, axis=-1, keepdims=True)


def seq_documents(docs_table, slot_index, span_order, span_len):
    docs_row = lax.dynamic_index_in_dim(docs_table, slot_index, 0, keepdims=False)
    return docs_row.reshape(-1, span_len)[span_order].reshape(-1)


def forward_layer(hidden, weight, positions, documents, ctx_rank, model_width):
    row_count = hidden.shape[0]
    qkv_cols = QH * HD + 2 * HD
    score_scale = HD ** (-0.5)
    hidden_f = hidden.astype(jnp.float32)
    partial_m = jnp.dot(hidden, weight[:, :qkv_cols], preferred_element_type=jnp.float32)
    partial_sq = jnp.sum(hidden_f * hidden_f, axis=1)
    merged, squares = lax.psum((partial_m, partial_sq), "tp")
    inv_rms = lax.rsqrt(squares / model_width + EPSILON)
    qkv = (inv_rms[:, None] * merged).astype(jnp.bfloat16)
    queries = qkv[:, : QH * HD].reshape(row_count, QH, HD)
    keys_own = qkv[:, QH * HD : QH * HD + HD]
    values_own = qkv[:, QH * HD + HD : qkv_cols]
    keys_all, values_all = (
        lax.all_gather(keys_own, "ctx", axis=0, tiled=True),
        lax.all_gather(values_own, "ctx", axis=0, tiled=True),
    )
    own_pos = lax.dynamic_slice_in_dim(positions, ctx_rank * row_count, row_count)
    own_doc = lax.dynamic_slice_in_dim(documents, ctx_rank * row_count, row_count)
    visible_mask = visible(own_pos, own_doc, positions, documents)
    scores = (
        jnp.einsum("qhc,kc->hqk", queries, keys_all, preferred_element_type=jnp.float32)
        * score_scale
    )
    attn_probs = softmax_rows(scores, visible_mask[None]).astype(jnp.bfloat16)
    attended = jnp.einsum("hqk,kc->qhc", attn_probs, values_all, preferred_element_type=jnp.float32)
    attended = attended.reshape(row_count, QH * HD).astype(jnp.bfloat16)
    update = jnp.einsum(
        "rc,dc->rd", attended, weight[:, qkv_cols:], preferred_element_type=jnp.float32
    )
    return (hidden_f + update).astype(jnp.bfloat16)


def backward_layer(stash_point, incoming, weight, positions, documents, ctx_rank, model_width):
    row_count = stash_point.shape[0]
    qkv_cols = QH * HD + 2 * HD
    score_scale = HD ** (-0.5)
    stash_f = stash_point.astype(jnp.float32)
    partial_m = jnp.dot(stash_point, weight[:, :qkv_cols], preferred_element_type=jnp.float32)
    partial_sq = jnp.sum(stash_f * stash_f, axis=1)
    partial_out = jnp.dot(incoming, weight[:, qkv_cols:], preferred_element_type=jnp.float32)
    merged, squares, out_sum = lax.psum((partial_m, partial_sq, partial_out), "tp")
    inv_rms = lax.rsqrt(squares / model_width + EPSILON)
    qkv = (inv_rms[:, None] * merged).astype(jnp.bfloat16)
    out_grad = out_sum.astype(jnp.bfloat16)
    query_flat = qkv[:, : QH * HD]
    keys_own = qkv[:, QH * HD : QH * HD + HD]
    values_own = qkv[:, QH * HD + HD : qkv_cols]
    keys_all, values_all = (
        lax.all_gather(keys_own, "ctx", axis=0, tiled=True),
        lax.all_gather(values_own, "ctx", axis=0, tiled=True),
    )
    row_start = ctx_rank * row_count
    query_heads = query_flat.reshape(row_count, QH, HD)
    out_heads = out_grad.reshape(row_count, QH, HD)
    own_pos = lax.dynamic_slice_in_dim(positions, row_start, row_count)
    own_doc = lax.dynamic_slice_in_dim(documents, row_start, row_count)
    visible_mask = visible(own_pos, own_doc, positions, documents)
    scores = (
        jnp.einsum("qhc,kc->hqk", query_heads, keys_all, preferred_element_type=jnp.float32)
        * score_scale
    )
    attn_probs = softmax_rows(scores, visible_mask[None])
    probs_low = attn_probs.astype(jnp.bfloat16)
    grad_prob = jnp.einsum("qhc,kc->hqk", out_heads, values_all, preferred_element_type=jnp.float32)
    delta_row = jnp.sum(attn_probs * grad_prob, axis=-1, keepdims=True)
    grad_score = (attn_probs * (grad_prob - delta_row) * score_scale).astype(jnp.bfloat16)
    grad_query = jnp.einsum("hqk,kc->qhc", grad_score, keys_all, preferred_element_type=jnp.float32)
    grad_query = grad_query.reshape(row_count, QH * HD)
    key_terms = jnp.einsum(
        "hqk,qhc->kc", grad_score, query_heads, preferred_element_type=jnp.float32
    )
    value_terms = jnp.einsum(
        "hqk,qhc->kc", probs_low, out_heads, preferred_element_type=jnp.float32
    )
    grad_key, grad_value = (
        lax.psum_scatter(key_terms, "ctx", scatter_dimension=0, tiled=True),
        lax.psum_scatter(value_terms, "ctx", scatter_dimension=0, tiled=True),
    )
    grad_qkv = jnp.concatenate([grad_query, grad_key, grad_value], axis=1).astype(jnp.bfloat16)
    grad_scale = jnp.sum(grad_qkv.astype(jnp.float32) * merged, axis=1)
    back_term = jnp.einsum(
        "rc,dc->rd", grad_qkv, weight[:, :qkv_cols], preferred_element_type=jnp.float32
    )
    result = incoming.astype(jnp.float32) + inv_rms[:, None] * back_term
    result = result - (inv_rms**3 * grad_scale / model_width)[:, None] * stash_f
    return result.astype(jnp.bfloat16)


def plain_body(fwd_acts, back_grads, stashed, layer_weights, span_order, fwd_docs, back_docs):
    sections = lax.axis_size("pipe")
    section_index = lax.axis_index("pipe")
    ctx_rank = lax.axis_index("ctx")
    row_count = fwd_acts.shape[1]
    span_len = row_count // SPANS
    model_width = fwd_acts.shape[2] * lax.axis_size("tp")
    tick_count = stashed.shape[1]
    offsets = jnp.arange(span_len, dtype=jnp.int32)
    positions = (span_order[:, None] * span_len + offsets[None, :]).reshape(-1)
    gathered = lax.all_gather(layer_weights, "ctx", axis=3, tiled=True)[:, 0]
    fwd_state = fwd_acts[0]
    back_state = back_grads[0]
    for tick_index in range(tick_count):
        fwd_slot = (section_index - tick_index) % sections
        fwd_half = jnp.where(section_index < tick_index, 1, 0)
        fwd_weight = lax.dynamic_index_in_dim(gathered, fwd_half, 0, keepdims=False)
        fwd_documents = seq_documents(fwd_docs, fwd_slot, span_order, span_len)
        fwd_state = forward_layer(
            fwd_state, fwd_weight, positions, fwd_documents, ctx_rank, model_width
        )
        fwd_state = from_behind(fwd_state, "pipe", 1)
        back_slot = (section_index + tick_index) % sections
        back_half = jnp.where(section_index + tick_index < sections, 1, 0)
        back_weight = lax.dynamic_index_in_dim(gathered, back_half, 0, keepdims=False)
        back_documents = seq_documents(back_docs, back_slot, span_order, span_len)
        back_state = backward_layer(
            stashed[0, tick_index],
            back_state,
            back_weight,
            positions,
            back_documents,
            ctx_rank,
            model_width,
        )
        back_state = from_behind(back_state, "pipe", -1)
    return (fwd_state[None], back_state[None])


QKV = QH * HD + 2 * HD
OC = QH * HD
WIDE = 256
DEPTHS = 4
KV_BLOCK = OC // WIDE
ORDER = (0, 1, KV_BLOCK, 2, 3)
MESH = pl.DeviceIdType.MESH
TRANS_B = (((1,), (1,)), ((), ()))
TRANS_A = (((0,), (0,)), ((), ()))


def dot_nt(a, b):
    return lax.dot_general(a, b, TRANS_B, preferred_element_type=jnp.float32)


def dot_tn(a, b):
    return lax.dot_general(a, b, TRANS_A, preferred_element_type=jnp.float32)


def dot_nn(a, b):
    return jnp.dot(a, b, preferred_element_type=jnp.float32)


class Place:
    def __init__(self, send_sem, recv_sem):
        self.p, self.c, self.t = (lax.axis_index(a) for a in ("pipe", "ctx", "tp"))
        self.n = lax.axis_size("tp")
        self.send_sem, self.recv_sem = send_sem, recv_sem

    def to(self, d):
        return lax.rem(self.t + d, self.n)

    def source(self, d):
        return lax.rem(self.t + self.n - d, self.n)

    def copy(self, src, dst, sem, c, t):
        return pltpu.make_async_remote_copy(
            src_ref=src,
            dst_ref=dst,
            send_sem=self.send_sem.at[sem],
            recv_sem=self.recv_sem.at[sem],
            device_id=(self.p, c, t),
            device_id_type=MESH,
        )

    def partner(self, src, dst, sem):
        return self.copy(src, dst, sem, 1 - self.c, self.t)

    def barrier(self):
        sem = pltpu.get_barrier_semaphore()
        for d in range(self.n):
            for other in (0, 1):
                if d == 0 and other == 0:
                    continue
                c = self.c if other == 0 else 1 - self.c
                pl.semaphore_signal(sem, inc=1, device_id=(self.p, c, self.to(d)), device_id_type=MESH)
        pl.semaphore_wait(sem, 2 * self.n - 1)


def row_squares(full, sq):
    @pl.loop(0, full.shape[0] // 32)
    def _(i):
        rows = pl.ds(pl.multiple_of(i * 32, 32), 32)
        x = full[rows, :].astype(jnp.float32)
        sq[rows, :] = jnp.broadcast_to(jnp.sum(x * x, axis=1, keepdims=True), (32, HD))


def project_block(pc, full, w, first, j, exact, part, landing, base, rows):
    cols = pl.ds(j * WIDE, WIDE)
    depth = full.shape[1] // DEPTHS
    exact[:, cols] = dot_nn(full[:, pl.ds(0, depth)], w[pl.ds(0, depth), pl.ds(first + j * WIDE, WIDE)])

    @pl.loop(1, DEPTHS)
    def _(i):
        deep = pl.ds(pl.multiple_of(i * depth, depth), depth)
        exact[:, cols] += dot_nn(full[:, deep], w[deep, pl.ds(first + j * WIDE, WIDE)])

    if part is None:
        part = exact
    else:
        part[:, cols] = exact[:, cols].astype(part.dtype)
    copies = []
    for d in range(1, pc.n):
        to = pc.to(d)
        mine = pl.ds(pl.multiple_of(to * rows, rows), rows)
        cp = pc.copy(part.at[mine, cols], landing.at[d - 1, :, cols], base + 3 * j + d - 1, pc.c, to)
        cp.start()
        copies.append(cp)
    return copies


def block_sum(pc, copies, j, exact, landing, rows):
    cols = pl.ds(j * WIDE, WIDE)
    total = exact[pl.ds(pl.multiple_of(pc.t * rows, rows), rows), cols]
    for d, cp in enumerate(copies):
        cp.wait_recv()
        total = total + landing[d, :, cols].astype(jnp.float32)
    return total


def scatter_start(pc, part, landing, cols, base, rows):
    copies = []
    for d in range(1, pc.n):
        to = pc.to(d)
        mine = pl.ds(pl.multiple_of(to * rows, rows), rows)
        cp = pc.copy(part.at[mine, pl.ds(0, cols)], landing.at[d - 1, :, pl.ds(0, cols)], base + d, pc.c, to)
        cp.start()
        copies.append(cp)
    return copies


def scatter_sum(pc, copies, part, landing, cols, rows):
    total = part[pl.ds(pl.multiple_of(pc.t * rows, rows), rows), pl.ds(0, cols)].astype(jnp.float32)
    for d, cp in enumerate(copies):
        cp.wait_recv()
        total = total + landing[d, :, pl.ds(0, cols)].astype(jnp.float32)
    for cp in copies:
        cp.wait_send()
    return total


def gather_start(pc, whole, base, rows, c, first=1):
    mine = pl.ds(pl.multiple_of(pc.t * rows, rows), rows)
    copies = []
    for d in range(first, pc.n):
        cp = pc.copy(whole.at[mine], whole.at[mine], base + d, c, pc.to(d))
        cp.start()
        copies.append(cp)
    return copies


def gather_wait(pc, whole, base, rows, first=1):
    for d in range(first, pc.n):
        there = pl.ds(pl.multiple_of(pc.source(d) * rows, rows), rows)
        pc.copy(whole.at[there], whole.at[there], base + d, pc.c, pc.source(d)).wait_recv()


def probabilities(q, k, seen):
    scores = dot_nt(q, k) * (HD ** (-0.5))
    masked = jnp.where(seen, scores, -jnp.inf)
    top = jnp.max(masked, axis=-1, keepdims=True)
    e = jnp.where(seen, jnp.exp(masked - top), 0.0)
    return e / jnp.sum(e, axis=-1, keepdims=True)


def qkv_rows(pc, width, full, w, ready, exact, landing, sq, sq_in, kv, m_ref, q_ref, rows):
    copies = {}
    for j in ORDER:
        ready(j)
        copies[j] = project_block(pc, full, w, 0, j, exact, None, landing, 40, rows)
        if j == KV_BLOCK:
            row_squares(full, sq)
            sq_copies = scatter_start(pc, sq, sq_in, HD, 4, rows)
    squares = scatter_sum(pc, sq_copies, sq, sq_in, HD, rows)
    r = lax.rsqrt(squares / width + EPSILON)
    mine = pl.ds(pl.multiple_of(pc.t * rows, rows), rows)
    for j in (KV_BLOCK, 0, 1, 2, 3):
        cols = pl.ds(j * WIDE, WIDE)
        m = block_sum(pc, copies[j], j, exact, landing, rows)
        if m_ref is not None:
            m_ref[:, cols] = m
        qkv = (r[:, :1] * m).astype(jnp.bfloat16)
        if j == KV_BLOCK:
            kv[mine, :] = qkv
            kv_copies = gather_start(pc, kv, 8, rows, 0)
        else:
            q_ref[:, cols] = qkv
    gather_wait(pc, kv, 8, rows)
    for cp in kv_copies + [cp for j in ORDER for cp in copies[j]]:
        cp.wait_send()
    return r


PIECES = 4


def hand_over(pc, stage, landed, out, base, make):
    span = out.shape[1] // PIECES
    copies = []
    for piece in range(PIECES):
        make(piece, span)
        cols = pl.ds(piece * span, span)
        cp = pc.partner(stage.at[:, cols], landed.at[:, cols], base + piece)
        cp.start()
        copies.append(cp)
    for cp in copies:
        cp.wait_send()


def take_over(pc, stage, landed, out, base):
    span = out.shape[1] // PIECES
    for piece in range(PIECES):
        cols = pl.ds(piece * span, span)
        pc.partner(stage.at[:, cols], landed.at[:, cols], base + piece).wait_recv()
        out[:, cols] = landed[:, cols]


def fetch_weight(pc, w_hbm, w, half, sem):
    copies = {}
    for j in ORDER:
        cols = pl.ds(j * WIDE, min(WIDE, w_hbm.shape[2] - j * WIDE))
        copies[j] = pltpu.make_async_copy(w_hbm.at[half, :, cols], w.at[:, cols], sem.at[j])
        copies[j].start()
    return copies


def values_weight(pc, w_hbm, w, half, sem):
    return pc.partner(w_hbm.at[half, :, pl.ds(0, HD)], w.at[:, pl.ds(QKV - HD, HD)], sem)


def forward_kernel(tick, width, seen_ref, h_ref, w_hbm, out_ref, w, full, exact, landing, sq, sq_in,
                   kv, q_ref, o_all, stage, landed, local_sem, send_sem, recv_sem):
    pc = Place(send_sem, recv_sem)
    own = h_ref.shape[0]
    rows = 2 * own // pc.n
    sections = lax.axis_size("pipe")
    half = (sections + tick - 1 - pc.p) // sections
    local = fetch_weight(pc, w_hbm, w, half, local_sem)
    pc.barrier()
    own_rows = pl.ds(pl.multiple_of(pc.c * own, own), own)
    hop = pc.partner(h_ref, full.at[own_rows], 0)
    hop.start()
    extra = values_weight(pc, w_hbm, w, half, 1)

    @pl.when(pc.c == 1)
    def _():
        extra.start()

    full[own_rows, :] = h_ref[...]
    other_rows = pl.ds(pl.multiple_of((1 - pc.c) * own, own), own)
    pc.partner(h_ref, full.at[other_rows], 0).wait_recv()

    @pl.when(pc.c == 0)
    def _():
        def ready(j):
            local[j].wait()
            if j == KV_BLOCK:
                extra.wait_recv()

        qkv_rows(pc, width, full, w, ready, exact, landing, sq, sq_in, kv, None, q_ref, rows)
        seen = seen_ref[...] > 0.0
        mine = pl.ds(pl.multiple_of(pc.t * rows, rows), rows)
        for h in range(QH):
            cols = pl.ds(h * HD, HD)
            p = probabilities(q_ref[:, cols], kv[:, pl.ds(0, HD)], seen).astype(jnp.bfloat16)
            o_all[mine, cols] = dot_nn(p, kv[:, pl.ds(HD, HD)]).astype(jnp.bfloat16)
        copies = gather_start(pc, o_all, 20, rows, 1, first=0)
        for cp in copies:
            cp.wait_send()
        take_over(pc, stage, landed, out_ref, 24)

    @pl.when(pc.c == 1)
    def _():
        extra.wait_send()
        for j in ORDER:
            local[j].wait()
        gather_wait(pc, o_all, 20, rows, first=0)

        def make(piece, span):
            @pl.loop(0, span // WIDE)
            def _(i):
                at = pl.multiple_of(piece * span + i * WIDE, WIDE)
                cols = pl.ds(at, WIDE)
                update = dot_nt(o_all[...], w[cols, pl.ds(HD, OC)])
                res = (full[:, cols].astype(jnp.float32) + update).astype(jnp.bfloat16)
                stage[:, cols] = res[:own]
                out_ref[:, cols] = res[own:]

        hand_over(pc, stage, landed, out_ref, 24, make)

    hop.wait_send()


def backward_kernel(tick, width, seen_ref, u_ref, g_ref, w_hbm, out_ref, w, full, gfull, exact, part, go_in, landing,
                    sq, sq_in, kv, q_ref, m_ref, go_ref, dkv, dkv_in, e_all, rc, stage, landed,
                    local_sem, send_sem, recv_sem):
    pc = Place(send_sem, recv_sem)
    own = u_ref.shape[0]
    rows = 2 * own // pc.n
    sections = lax.axis_size("pipe")
    half = (2 * sections - 1 - pc.p - tick) // sections
    local = fetch_weight(pc, w_hbm, w, half, local_sem)
    pc.barrier()
    own_rows = pl.ds(pl.multiple_of(pc.c * own, own), own)
    other_rows = pl.ds(pl.multiple_of((1 - pc.c) * own, own), own)
    extra = values_weight(pc, w_hbm, w, half, 1)
    uhop = pc.partner(u_ref, full.at[own_rows], 0)
    ghop = pc.partner(g_ref, gfull.at[own_rows], 2)

    @pl.when(pc.c == 1)
    def _():
        uhop.start()
        extra.start()

    ghop.start()
    gfull[own_rows, :] = g_ref[...]

    @pl.when(pc.c == 0)
    def _():
        full[own_rows, :] = u_ref[...]
        pc.partner(u_ref, full.at[other_rows], 0).wait_recv()

        def ready(j):
            local[j].wait()
            if j == KV_BLOCK:
                extra.wait_recv()

        r = qkv_rows(pc, width, full, w, ready, exact, landing, sq, sq_in, kv, m_ref, q_ref, rows)
        pc.partner(go_ref, go_ref, 3).wait_recv()
        seen = seen_ref[...] > 0.0
        mine = pl.ds(pl.multiple_of(pc.t * rows, rows), rows)
        k, v = kv[:, pl.ds(0, HD)], kv[:, pl.ds(HD, HD)]
        dr = jnp.zeros((rows, 1), jnp.float32)
        dk = jnp.zeros((2 * own, HD), jnp.float32)
        dv = jnp.zeros((2 * own, HD), jnp.float32)
        for h in range(QH):
            cols = pl.ds(h * HD, HD)
            q, go = q_ref[:, cols], go_ref[:, cols]
            p = probabilities(q, k, seen)
            dp = dot_nt(go, v)
            delta = jnp.sum(p * dp, axis=-1, keepdims=True)
            ds = (p * (dp - delta) * (HD ** (-0.5))).astype(jnp.bfloat16)
            dq = dot_nn(ds, k).astype(jnp.bfloat16)
            e_all[mine, cols] = dq
            dr = dr + jnp.sum(dq.astype(jnp.float32) * m_ref[:, cols], axis=1, keepdims=True)
            dk = dk + dot_tn(ds, q)
            dv = dv + dot_tn(p.astype(jnp.bfloat16), go)
        dkv[:, pl.ds(0, HD)] = dk
        dkv[:, pl.ds(HD, HD)] = dv
        copies = scatter_start(pc, dkv, dkv_in, 2 * HD, 24, rows)
        last = scatter_sum(pc, copies, dkv, dkv_in, 2 * HD, rows).astype(jnp.bfloat16)
        e_all[mine, pl.ds(OC, 2 * HD)] = last
        dr = dr + jnp.sum(last.astype(jnp.float32) * m_ref[:, pl.ds(OC, 2 * HD)], axis=1, keepdims=True)
        lane = lax.broadcasted_iota(jnp.int32, (rows, HD), 1)
        rc[mine, :] = jnp.where(lane < HD // 2, r, r * r * r * dr / width)
        copies = gather_start(pc, e_all, 28, rows, 0) + gather_start(pc, rc, 32, rows, 0)
        gather_wait(pc, e_all, 28, rows)
        gather_wait(pc, rc, 32, rows)
        for cp in copies:
            cp.wait_send()
        pc.partner(g_ref, gfull.at[other_rows], 2).wait_recv()

        def make(piece, span):
            @pl.loop(0, span // WIDE)
            def _(i):
                at = pl.multiple_of(piece * span + i * WIDE, WIDE)
                cols = pl.ds(at, WIDE)
                back = dot_nt(e_all[...], w[cols, :])
                res = gfull[:, cols].astype(jnp.float32) + rc[:, pl.ds(0, 1)] * back
                res = res - rc[:, pl.ds(HD // 2, 1)] * full[:, cols].astype(jnp.float32)
                res = res.astype(jnp.bfloat16)
                out_ref[:, cols] = res[:own]
                stage[:, cols] = res[own:]

        hand_over(pc, stage, landed, out_ref, 36, make)

    @pl.when(pc.c == 1)
    def _():
        pc.partner(g_ref, gfull.at[other_rows], 2).wait_recv()
        for j in ORDER:
            local[j].wait()
        copies = [project_block(pc, gfull, w, HD, j, exact, part, go_in, 60, rows) for j in range(KV_BLOCK)]
        for j in range(KV_BLOCK):
            go_ref[:, pl.ds(j * WIDE, WIDE)] = block_sum(pc, copies[j], j, exact, go_in, rows).astype(jnp.bfloat16)
        for group in copies:
            for cp in group:
                cp.wait_send()
        give = pc.partner(go_ref, go_ref, 3)
        give.start()
        give.wait_send()
        uhop.wait_send()
        extra.wait_send()
        take_over(pc, stage, landed, out_ref, 36)

    ghop.wait_send()


def call(kernel, collective_id, operands, specs, like, scratch, flops):
    return pl.pallas_call(
        kernel,
        out_shape=jax.ShapeDtypeStruct(like.shape, like.dtype),
        in_specs=specs,
        out_specs=pl.BlockSpec(memory_space=pltpu.VMEM),
        scratch_shapes=scratch + [pltpu.SemaphoreType.DMA((KV_BLOCK + 1,)), pltpu.SemaphoreType.DMA((72,)), pltpu.SemaphoreType.DMA((72,))],
        compiler_params=pltpu.CompilerParams(
            collective_id=collective_id, has_side_effects=True, vmem_limit_bytes=48 * 2**20
        ),
        cost_estimate=pl.CostEstimate(flops=flops, bytes_accessed=12 * 2**20, transcendentals=0),
    )(*operands)


def fused_body(fwd_acts, back_grads, stashed, layer_weights, span_order, fwd_docs, back_docs):
    sections, n = lax.axis_size("pipe"), lax.axis_size("tp")
    p, t = lax.axis_index("pipe"), lax.axis_index("tp")
    own, model = fwd_acts.shape[1:]
    seq = 2 * own
    rows = seq // n
    span = own // SPANS
    width = model * n
    ticks = stashed.shape[1]
    offsets = jnp.arange(span, dtype=jnp.int32)
    positions = (span_order[:, None] * span + offsets[None, :]).reshape(-1)
    weights = layer_weights[:, 0]
    bf, f32 = jnp.bfloat16, jnp.float32
    vm = pltpu.VMEM
    shared = [
        vm((seq, QKV), f32), vm((n - 1, rows, QKV), f32), vm((seq, HD), f32),
        vm((n - 1, rows, HD), f32), vm((seq, 2 * HD), bf), vm((rows, OC), bf),
    ]
    edge = [vm((own, model), bf), vm((own, model), bf)]
    fwd_scratch = [vm((model, QKV), bf), vm((seq, model), bf)] + shared + [vm((seq, OC), bf)] + edge
    back_scratch = [vm((model, QKV), bf), vm((seq, model), bf), vm((seq, model), bf), shared[0],
                    vm((seq, OC), bf), vm((n - 1, rows, OC), bf)] + shared[1:] + [
        vm((rows, QKV), f32), vm((rows, OC), bf), vm((seq, 2 * HD), f32), vm((n - 1, rows, 2 * HD), f32),
        vm((seq, QKV), bf), vm((seq, HD), f32)] + edge
    in_vmem = pl.BlockSpec(memory_space=pltpu.VMEM)
    anywhere = pl.BlockSpec(memory_space=pl.ANY)

    def seen(docs, slot):
        documents = seq_documents(docs, slot, span_order, span)
        my_pos = lax.dynamic_slice_in_dim(positions, t * rows, rows)
        my_doc = lax.dynamic_slice_in_dim(documents, t * rows, rows)
        return visible(my_pos, my_doc, positions, documents).astype(f32)

    fwd, back = fwd_acts[0], back_grads[0]
    for tick in range(ticks):
        fwd_seen = seen(fwd_docs, (p - tick) % sections)
        fwd = call(functools.partial(forward_kernel, tick, width), tick, (fwd_seen, fwd, weights),
                   [in_vmem, in_vmem, anywhere], fwd, fwd_scratch, 3 * 10**10)
        fwd = from_behind(fwd, "pipe", 1)
        back_seen = seen(back_docs, (p + tick) % sections)
        back = call(functools.partial(backward_kernel, tick, width), ticks + tick,
                    (back_seen, stashed[0, tick], back, weights),
                    [in_vmem, in_vmem, in_vmem, anywhere], back, back_scratch, 3 * 10**10)
        back = from_behind(back, "pipe", -1)
    return (fwd[None], back[None])


def solution(mesh):
    return jax.shard_map(
        fused_body if mesh.shape["tp"] <= 4 else plain_body,
        mesh=mesh,
        in_specs=(
            P("pipe", "ctx", "tp"),
            P("pipe", "ctx", "tp"),
            P("pipe", None, "ctx", "tp"),
            P(None, "pipe", "tp", "ctx"),
            P(),
            P(),
            P(),
        ),
        out_specs=(P("pipe", "ctx", "tp"), P("pipe", "ctx", "tp")),
        check_vma=False,
    )
```
